256 devices in a mesh: pix: 16 (over y, x_hi, core), tm: 16 (over x_lo, z).
Axes of the slice: x: 4 (x_hi: 2, x_lo: 2; x = x_hi * 2 + x_lo), y: 4, z: 8, core: 2. Of those that a mesh axis runs over, the one named last changes fastest.
Arguments:
- raw_movie: float32 [128, 256, 8192], P('pix', None, 'tm'), may hold values from 0.05 to 2
- footprints: float32 [256, 32768], P('tm', 'pix'), may hold values from 0.05 to 1
- traces: float32 [256, 8192], P('pix', 'tm'), may hold values from 0.05 to 1
Outputs:
- denoised: float32 [128, 256, 8192], P('pix', None, 'tm')
- new_footprints: float32 [256, 32768], P('tm', 'pix')
- new_traces: float32 [256, 8192], P('pix', 'tm')
The draws below stay inside these ranges and needn't reach their ends.
All inputs are finite; a program needn't handle non-finite values.
Results may differ from the reference program's by a relative error of at most 0.00013.
Values sent between devices are 32-bit elements; how exact they have to be, the bound alone decides.
A program may use at most 64 MiB of HBM per device.

```python
import math
import jax
import jax.numpy as jnp
from jax import lax

WID = 256
FR_DEV = 512
RANK = 256
HGT = 128
PIXELS = 32768
FRAMES = 8192
N_TM = 16


def block_scale(key, dims, cuts, least, largest):
    def one(position, shards_of):
        draws = jax.random.uniform(jax.random.fold_in(jax.random.fold_in(key, 6), position), (shards_of,), jnp.float32, least / len(cuts), largest / len(cuts))
        return jnp.repeat(jnp.exp(draws), dims[position] // shards_of).reshape((-1,) + (1,) * (len(dims) - position - 1))

    loudness = one(*cuts[0])
    for cut in cuts[1:]:
        loudness = loudness * one(*cut)
    return loudness


def setup_inputs(seed: int = 0) -> dict:
    keys = jax.random.split(jax.random.key(seed), 4)
    raw_movie = jnp.clip(jnp.exp(math.log(2.0) - 3.6888794 * jax.random.uniform(keys[0], (HGT, WID, FRAMES), jnp.float32) ** block_scale(keys[0], (HGT, WID, FRAMES), ((0, 16), (2, 16)), -0.2, 0.2)), 0.05, 2.0)
    footprints = jnp.clip(jnp.exp(math.log(1.0) - 2.9957323 * jax.random.uniform(keys[1], (RANK, PIXELS), jnp.float32) ** block_scale(keys[1], (RANK, PIXELS), ((0, 16), (1, 16)), -0.2, 0.2)), 0.05, 1.0)
    traces = jnp.clip(jnp.exp(math.log(1.0) - 2.9957323 * jax.random.uniform(keys[2], (RANK, FRAMES), jnp.float32) ** block_scale(keys[2], (RANK, FRAMES), ((0, 16), (1, 16)), -0.2, 0.2)), 0.05, 1.0)
    return {"raw_movie": raw_movie, "footprints": footprints, "traces": traces}


edge_scale = 0.5
step_size = 0.24


def flux_term(change):
    return change / (1.0 + (change / edge_scale) * (change / edge_scale))


def substep(extended):
    middle = extended[1:-1]
    padded = jnp.pad(middle, ((0, 0), (1, 1), (0, 0)))
    summed = flux_term(extended[:-2] - middle) + flux_term(extended[2:] - middle)
    summed = summed + flux_term(padded[:, :-2] - middle) + flux_term(padded[:, 2:] - middle)
    return middle + step_size * summed


def diffuse(frames_block):
    current = frames_block
    for repeat in range(4):
        current = substep(jnp.pad(current, ((1, 1), (0, 0), (0, 0))))
    return current


def matmul_hi(left, right):
    return jnp.dot(left, right, precision=lax.Precision.HIGHEST, preferred_element_type=jnp.float32)


def contract_last(left, right):
    return lax.dot_general(left, right, (((1,), (1,)), ((), ())), precision=lax.Precision.HIGHEST, preferred_element_type=jnp.float32)


def reference(raw_movie, footprints, traces):
    stacked = jnp.moveaxis(raw_movie.reshape(HGT, WID, N_TM, FR_DEV), 2, 0)
    denoised = jnp.moveaxis(lax.map(diffuse, stacked), 0, 2).reshape(HGT, WID, FRAMES)
    pixels = denoised.reshape(HGT * WID, FRAMES)
    numerator = matmul_hi(footprints, pixels)
    gram = contract_last(footprints, footprints)
    new_traces = traces * numerator / matmul_hi(gram, traces)
    foot_numerator = contract_last(new_traces, pixels)
    trace_gram = contract_last(new_traces, new_traces)
    new_footprints = footprints * foot_numerator / matmul_hi(trace_gram, footprints)
    return denoised, new_footprints, new_traces
```

```python
import jax
import jax.numpy as jnp
from jax import lax
from jax.experimental import pallas as pl
from jax.experimental.pallas import tpu as pltpu
from jax.sharding import PartitionSpec as P

F32 = jnp.float32
BF16 = jnp.bfloat16
MESH = pl.DeviceIdType.MESH
HALO = 4
ROWS = 8
EXT = ROWS + 2 * HALO
COLS = 256
FRAMES = 512
CHUNK = 128
CHUNKS = FRAMES // CHUNK
RANK = 256
BLK = 16
NB = RANK // BLK
CHIPS = 8
NPIX = 16
NZ = 8
LOCAL = ROWS * COLS
WIDE = LOCAL + RANK
STEP = 0.24


def split(x):
    hi = x.astype(BF16)
    return hi, (x - hi.astype(F32)).astype(BF16)


def dot3(ah, al, bh, bl, rhs_dim):
    dims = (((1,), (rhs_dim,)), ((), ()))

    def one(a, b):
        return lax.dot_general(a, b, dims, preferred_element_type=F32)

    return one(ah, bh) + (one(al, bh) + one(ah, bl))


def flux_den(c):
    return 1.0 + 4.0 * (c * c)


def kernel(
    raw, foot, traces, den_out, foot_out, trace_out,
    y_buf, fd_buf, ph, plo, ff, fh8, fl8, fn, lu, ld, lx, gp, gcr, gl, tf, scale_buf,
    np_buf, cr_buf, lc_buf, nf,
    loc_sem, out_sem, halo_s, halo_r, fx_s, fx_r, fr_s, fr_r, ring_s, ring_r, rx_s, rx_r,
    core_s, core_r, chip_s, chip_r,
):
    p = lax.axis_index("pix")
    t = lax.axis_index("tm")
    chip = p // 2
    core = p % 2
    xl = t // NZ
    z = t % NZ
    up = (p, xl * NZ + (z + 1) % NZ)
    down = (p, xl * NZ + (z + NZ - 1) % NZ)
    across = (p, (1 - xl) * NZ + z)
    sibling = (chip * 2 + (1 - core), t)
    pending = []

    def remote(src, dst, ssem, rsem, dev):
        return pltpu.make_async_remote_copy(
            src_ref=src, dst_ref=dst, send_sem=ssem, recv_sem=rsem, device_id=dev, device_id_type=MESH
        )

    def send(*args):
        cp = remote(*args)
        cp.start()
        pending.append(cp)
        return cp

    def peer_chip(i):
        return ((lax.rem(chip + i, CHIPS)) * 2 + core, t)

    loads = []
    for c in range(CHUNKS):
        cp = pltpu.make_async_copy(
            raw.at[:, :, pl.ds(c * CHUNK, CHUNK)], y_buf.at[c, pl.ds(HALO, ROWS)], loc_sem.at[c]
        )
        cp.start()
        loads.append(cp)
    foot_load = pltpu.make_async_copy(foot, ff.at[t], loc_sem.at[CHUNKS])
    foot_load.start()
    trace_load = pltpu.make_async_copy(traces, tf.at[chip, core], loc_sem.at[CHUNKS + 1])
    trace_load.start()

    halo_far = (lax.rem(p + NPIX + 2 * core - 1, NPIX), t)
    partners = [sibling, halo_far, across, up, down] + [peer_chip(i) for i in range(1, CHIPS)]
    bar = pltpu.get_barrier_semaphore()
    for dev in partners:
        pl.semaphore_signal(bar, inc=1, device_id=dev, device_id_type=MESH)

    @pl.when(p == 0)
    def _():
        for c in range(CHUNKS):
            y_buf[c, pl.ds(0, HALO)] = jnp.zeros((HALO, COLS, CHUNK), F32)

    @pl.when(p == NPIX - 1)
    def _():
        for c in range(CHUNKS):
            y_buf[c, pl.ds(HALO + ROWS, HALO)] = jnp.zeros((HALO, COLS, CHUNK), F32)

    pl.semaphore_wait(bar, len(partners))

    def halo_down(c):
        return remote(
            raw.at[pl.ds(ROWS - HALO, HALO), :, pl.ds(c * CHUNK, CHUNK)],
            y_buf.at[c, pl.ds(0, HALO)], halo_s.at[0, c], halo_r.at[0, c],
            (lax.rem(p + 1, NPIX), t),
        )

    def halo_up(c):
        return remote(
            raw.at[pl.ds(0, HALO), :, pl.ds(c * CHUNK, CHUNK)],
            y_buf.at[c, pl.ds(HALO + ROWS, HALO)], halo_s.at[1, c], halo_r.at[1, c],
            (lax.rem(p + NPIX - 1, NPIX), t),
        )

    def halo_start(c):
        @pl.when(p < NPIX - 1)
        def _():
            halo_down(c).start()

        @pl.when(p > 0)
        def _():
            halo_up(c).start()

    def halo_wait(c):
        @pl.when(p > 0)
        def _():
            halo_down(c).wait_recv()

        @pl.when(p < NPIX - 1)
        def _():
            halo_up(c).wait_recv()

    def halo_wait_send(c):
        @pl.when(p < NPIX - 1)
        def _():
            halo_down(c).wait_send()

        @pl.when(p > 0)
        def _():
            halo_up(c).wait_send()

    def fblock(j, dz):
        col = xl if j == 1 else 1 - xl
        return col * NZ + lax.rem(z + dz + 2 * NZ, NZ)

    def foot_send(s, j):
        cps = []
        for d in range(2):
            if s == 3 and d == j:
                continue
            sign = -1 if d == 0 else 1
            b = fblock(j, sign * s)
            src = foot if (s == 0 and j == 1) else ff.at[b]
            cps.append(send(src, ff.at[b], fr_s.at[d, s, j], fr_r.at[d, s, j], up if d == 0 else down))
        return cps

    def wait_all(cps):
        for cp in cps:
            cp.wait_recv()

    def gather_chips(src, dst, slot):
        cps = []
        for i in range(1, CHIPS):
            cps.append(send(src, dst, chip_s.at[slot, i], chip_r.at[slot, i], peer_chip(i)))
        return cps

    def diffuse(c):
        def substep(s, carry):
            src = jnp.where(lax.rem(s, 2) == 1, c, CHUNKS)
            dst = jnp.where(lax.rem(s, 2) == 1, CHUNKS, c)
            col = lax.broadcasted_iota(jnp.int32, (COLS, CHUNK), 0)
            first = s - 1
            c0 = y_buf[src, first + 1] - y_buf[src, first]
            fd_buf[...] = c0 / flux_den(c0)

            def row(r, carry):
                u = y_buf[src, r]
                cd = y_buf[src, r + 1] - u
                ur = jnp.where(col == COLS - 1, 0.0, pltpu.roll(u, COLS - 1, 0))
                cr = ur - u
                dd = flux_den(cd)
                dr = flux_den(cr)
                inv = 1.0 / (dd * dr)
                fdn = cd * (dr * inv)
                frt = cr * (dd * inv)
                u0 = u[0:8]
                edge = u0 / flux_den(u0)
                edge = jnp.concatenate([edge, frt[8:]], axis=0)
                fl = jnp.where(col == 0, edge, pltpu.roll(frt, 1, 0))
                total = (fdn - fd_buf[...]) + (frt - fl)
                fd_buf[...] = fdn
                new = u + STEP * total
                outside = ((p == 0) & (r < HALO)) | ((p == NPIX - 1) & (r >= HALO + ROWS))
                y_buf[dst, r] = jnp.where(outside, 0.0, new)
                return carry

            return lax.fori_loop(s, EXT - s, row, carry)

        lax.fori_loop(1, HALO + 1, substep, 0)
        for r in range(ROWS):
            hi, lo = split(y_buf[c, HALO + r])
            ph[c, r] = hi
            plo[c, r] = lo

    def numerator(c):
        def body(r, acc):
            return acc + dot3(fh8[r], fl8[r], ph[c, r], plo[c, r], 0)

        part = lax.fori_loop(0, ROWS, body, jnp.zeros((RANK, CHUNK), F32))
        np_buf[c] = part.reshape(CHIPS, 2, BLK, CHUNK)

    def rs_core(c):
        return send(np_buf.at[c, :, 1 - core], cr_buf.at[c], core_s.at[c], core_r.at[c], sibling)

    def rs_chips(c, cp):
        cp.wait_recv()
        cr_buf[c] = cr_buf[c] + np_buf[c, :, core]
        cps = []
        for i in range(1, CHIPS):
            cps.append(
                send(
                    cr_buf.at[c, lax.rem(chip + i, CHIPS)], lc_buf.at[c, i],
                    chip_s.at[c, i], chip_r.at[c, i], peer_chip(i),
                )
            )
        return cps

    def ag_chips(c, cps):
        wait_all(cps)
        num = cr_buf[c, chip]
        for i in range(1, CHIPS):
            num = num + lc_buf[c, i]
        new = num * scale_buf[:, c * CHUNK : (c + 1) * CHUNK]
        trace_out[:, c * CHUNK : (c + 1) * CHUNK] = new
        nf[c, chip, core] = new
        return gather_chips(nf.at[c, chip, core], nf.at[c, chip, core], CHUNKS + c)

    def ag_core(c, cps):
        wait_all(cps)
        return send(
            nf.at[c, :, core], nf.at[c, :, core], core_s.at[CHUNKS + c], core_r.at[CHUNKS + c], sibling
        )

    def foot_update(c, cp):
        cp.wait_recv()
        nh, nl = split(nf[c].reshape(RANK, CHUNK))
        first = c == 0

        def put(where, val):
            val = val.reshape(NB, BLK, RANK)
            fn[:, :, where] = val if first else fn[:, :, where] + val

        put(pl.ds(LOCAL, RANK), dot3(nh, nl, nh, nl, 1))

        def body(r, carry):
            put(pl.ds(pl.multiple_of(r * COLS, COLS), COLS), dot3(nh, nl, ph[c, r], plo[c, r], 1))
            return carry

        lax.fori_loop(0, ROWS, body, 0)

    halo_start(0)
    fx = send(foot, ff.at[t], fx_s.at[0], fx_r.at[0], across)
    own0 = foot_send(0, 1)
    tr = gather_chips(traces, tf.at[chip, core], 2 * CHUNKS)
    halo_start(1)
    fx.wait_recv()
    oth0 = foot_send(0, 0)
    wait_all(own0)
    own1 = foot_send(1, 1)
    wait_all(oth0)
    oth1 = foot_send(1, 0)
    wait_all(tr)
    trace_load.wait()
    tr_core = send(tf.at[:, core], tf.at[:, core], core_s.at[2 * CHUNKS], core_r.at[2 * CHUNKS], sibling)
    wait_all(own1)
    own2 = foot_send(2, 1)
    wait_all(oth1)
    oth2 = foot_send(2, 0)
    for cp in loads:
        cp.wait()
    halo_wait(0)
    halo_start(2)
    diffuse(0)
    stores = []

    def store(c):
        cp = pltpu.make_async_copy(
            y_buf.at[c, pl.ds(HALO, ROWS)], den_out.at[:, :, pl.ds(c * CHUNK, CHUNK)], out_sem.at[c]
        )
        cp.start()
        stores.append(cp)

    store(0)
    wait_all(own2)
    own3 = foot_send(3, 1)
    wait_all(oth2)
    oth3 = foot_send(3, 0)
    foot_load.wait()
    halo_wait(1)
    halo_start(3)
    diffuse(1)
    store(1)
    wait_all(own3)
    wait_all(oth3)

    def split_foot(r, carry):
        hi, lo = split(ff[:, :, pl.ds(pl.multiple_of(r * COLS, COLS), COLS)].reshape(RANK, COLS))
        fh8[r] = hi
        fl8[r] = lo
        return carry

    lax.fori_loop(0, ROWS, split_foot, 0)

    def gram_body(r, acc):
        return acc + dot3(fh8[r], fl8[r], fh8[r], fl8[r], 1)

    gp[...] = lax.fori_loop(0, ROWS, gram_body, jnp.zeros((RANK, RANK), F32)).reshape(CHIPS, 2, BLK, RANK)
    gslot = 2 * CHUNKS + 1
    g_core = send(gp.at[:, 1 - core], gcr, core_s.at[gslot], core_r.at[gslot], sibling)
    numerator(0)
    rs0 = rs_core(0)
    g_core.wait_recv()
    gcr[...] = gcr[...] + gp[:, core]
    g_chips = []
    for i in range(1, CHIPS):
        g_chips.append(
            send(gcr.at[lax.rem(chip + i, CHIPS)], gl.at[i], chip_s.at[gslot, i], chip_r.at[gslot, i], peer_chip(i))
        )
    rs0 = rs_chips(0, rs0)
    numerator(1)
    rs1 = rs_core(1)
    rs1 = rs_chips(1, rs1)
    wait_all(g_chips)
    gram = gcr[chip]
    for i in range(1, CHIPS):
        gram = gram + gl[i]
    tr_core.wait_recv()
    gh, gl_ = split(gram)
    th, tl = split(tf[...].reshape(RANK, FRAMES))
    scale_buf[...] = tf[chip, core] / dot3(gh, gl_, th, tl, 0)
    ag0 = ag_chips(0, rs0)
    halo_wait(2)
    diffuse(2)
    store(2)
    ag0 = ag_core(0, ag0)
    ag1 = ag_chips(1, rs1)
    numerator(2)
    rs2 = rs_core(2)
    foot_update(0, ag0)
    rs2 = rs_chips(2, rs2)
    ag1 = ag_core(1, ag1)
    foot_update(1, ag1)
    halo_wait(3)
    diffuse(3)
    store(3)
    ag2 = ag_chips(2, rs2)
    numerator(3)
    rs3 = rs_core(3)
    rs3 = rs_chips(3, rs3)
    ag2 = ag_core(2, ag2)
    foot_update(2, ag2)
    ag3 = ag_chips(3, rs3)
    ag3 = ag_core(3, ag3)
    foot_update(3, ag3)

    def ring_send(s, j, got):
        cps = []
        for d in range(2):
            if s == 0 and d == j:
                continue
            land = lu if d == 0 else ld
            b = fblock(j, (NZ // 2 - s) * (1 if d == 0 else -1))
            if d in got:
                land[s - 1, j] = land[s - 1, j] + fn[b]
                src = land.at[s - 1, j]
            else:
                src = fn.at[b]
            cps.append(send(src, land.at[s, j], ring_s.at[d, s, j], ring_r.at[d, s, j], up if d == 0 else down))
        return cps

    r0 = ring_send(0, 0, ())
    r1 = ring_send(0, 1, ())
    for s in range(1, 4):
        wait_all(r0)
        r0 = ring_send(s, 0, (1,) if s == 1 else (0, 1))
        wait_all(r1)
        r1 = ring_send(s, 1, (0,) if s == 1 else (0, 1))
    wait_all(r0)
    bo = fblock(0, 0)
    lu[3, 0] = (lu[3, 0] + ld[3, 0]) + fn[bo]
    rx = send(lu.at[3, 0], lx, rx_s.at[0], rx_r.at[0], across)
    wait_all(r1)
    lu[3, 1] = (lu[3, 1] + ld[3, 1]) + fn[fblock(1, 0)]
    rx.wait_recv()
    kh, kl = split(lu[3, 1, :, pl.ds(LOCAL, RANK)] + lx[:, pl.ds(LOCAL, RANK)])

    def final(r, carry):
        w = pl.ds(pl.multiple_of(r * COLS, COLS), COLS)
        den = dot3(kh, kl, fh8[r], fl8[r], 0)
        foot_out[:, w] = ff[t, :, w] * (lu[3, 1, :, w] + lx[:, w]) / den
        return carry

    lax.fori_loop(0, ROWS, final, 0)

    for cp in pending:
        cp.wait_send()
    for c in range(CHUNKS):
        halo_wait_send(c)
    for cp in stores:
        cp.wait()


def body(raw_movie, footprints, traces):
    dma = pltpu.SemaphoreType.DMA
    vm = pltpu.VMEM
    hbm = pl.BlockSpec(memory_space=pltpu.MemorySpace.HBM)
    inv = pl.BlockSpec(memory_space=pltpu.MemorySpace.VMEM)
    return pl.pallas_call(
        kernel,
        out_shape=(
            jax.ShapeDtypeStruct(raw_movie.shape, F32),
            jax.ShapeDtypeStruct(footprints.shape, F32),
            jax.ShapeDtypeStruct(traces.shape, F32),
        ),
        in_specs=[hbm, hbm, hbm],
        out_specs=(hbm, inv, inv),
        scratch_shapes=[
            vm((CHUNKS + 1, EXT, COLS, CHUNK), F32),
            vm((COLS, CHUNK), F32),
            vm((CHUNKS, ROWS, COLS, CHUNK), BF16),
            vm((CHUNKS, ROWS, COLS, CHUNK), BF16),
            vm((NB, BLK, LOCAL), F32),
            vm((ROWS, RANK, COLS), BF16),
            vm((ROWS, RANK, COLS), BF16),
            vm((NB, BLK, WIDE), F32),
            vm((4, 2, BLK, WIDE), F32),
            vm((4, 2, BLK, WIDE), F32),
            vm((BLK, WIDE), F32),
            vm((CHIPS, 2, BLK, RANK), F32),
            vm((CHIPS, BLK, RANK), F32),
            vm((CHIPS, BLK, RANK), F32),
            vm((CHIPS, 2, BLK, FRAMES), F32),
            vm((BLK, FRAMES), F32),
            vm((CHUNKS, CHIPS, 2, BLK, CHUNK), F32),
            vm((CHUNKS, CHIPS, BLK, CHUNK), F32),
            vm((CHUNKS, CHIPS, BLK, CHUNK), F32),
            vm((CHUNKS, CHIPS, 2, BLK, CHUNK), F32),
            dma((CHUNKS + 2,)),
            dma((CHUNKS,)),
            dma((2, CHUNKS)),
            dma((2, CHUNKS)),
            dma((1,)),
            dma((1,)),
            dma((2, 4, 2)),
            dma((2, 4, 2)),
            dma((2, 4, 2)),
            dma((2, 4, 2)),
            dma((1,)),
            dma((1,)),
            dma((2 * CHUNKS + 2,)),
            dma((2 * CHUNKS + 2,)),
            dma((2 * CHUNKS + 2, CHIPS)),
            dma((2 * CHUNKS + 2, CHIPS)),
        ],
        compiler_params=pltpu.CompilerParams(
            collective_id=0, has_side_effects=True, vmem_limit_bytes=48 * 1024 * 1024
        ),
        cost_estimate=pl.CostEstimate(flops=4 * 10**9, bytes_accessed=16 * 2**20, transcendentals=0),
    )(raw_movie, footprints, traces)


def solution(mesh):
    placed = (P("pix", None, "tm"), P("tm", "pix"), P("pix", "tm"))
    return jax.shard_map(body, mesh=mesh, in_specs=placed, out_specs=placed, check_vma=False)
```

```python
import jax
import jax.numpy as jnp
from jax import lax
from jax.experimental import pallas as pl
from jax.experimental.pallas import tpu as pltpu
from jax.sharding import PartitionSpec as P

F32 = jnp.float32
BF16 = jnp.bfloat16
MESH = pl.DeviceIdType.MESH
HALO = 4
ROWS = 8
EXT = ROWS + 2 * HALO
COLS = 256
FRAMES = 512
CHUNK = 128
CHUNKS = FRAMES // CHUNK
RANK = 256
BLK = 16
NB = RANK // BLK
CHIPS = 8
NPIX = 16
NZ = 8
LOCAL = ROWS * COLS
WIDE = LOCAL + RANK
STEP = 0.24


def split(x):
    hi = x.astype(BF16)
    return hi, (x - hi.astype(F32)).astype(BF16)


def dot3(ah, al, bh, bl, rhs_dim):
    dims = (((1,), (rhs_dim,)), ((), ()))

    def one(a, b):
        return lax.dot_general(a, b, dims, preferred_element_type=F32)

    return one(ah, bh) + (one(al, bh) + one(ah, bl))


def flux_den(c):
    return 1.0 + 4.0 * (c * c)


def kernel(
    raw, foot, traces, den_out, foot_out, trace_out,
    y_buf, fd_buf, ph, plo, ff, fh8, fl8, fn, lu, ld, lx, gp, gcr, gl, tf, scale_buf,
    np_buf, cr_buf, lc_buf, nf, pth, ptl,
    loc_sem, out_sem, halo_s, halo_r, fx_s, fx_r, fr_s, fr_r, ring_s, ring_r, rx_s, rx_r,
    core_s, core_r, chip_s, chip_r,
):
    p = lax.axis_index("pix")
    t = lax.axis_index("tm")
    chip = p // 2
    core = p % 2
    xl = t // NZ
    z = t % NZ
    up = (p, xl * NZ + (z + 1) % NZ)
    down = (p, xl * NZ + (z + NZ - 1) % NZ)
    across = (p, (1 - xl) * NZ + z)
    sibling = (chip * 2 + (1 - core), t)
    pending = []

    def remote(src, dst, ssem, rsem, dev):
        return pltpu.make_async_remote_copy(
            src_ref=src, dst_ref=dst, send_sem=ssem, recv_sem=rsem, device_id=dev, device_id_type=MESH
        )

    def send(*args):
        cp = remote(*args)
        cp.start()
        pending.append(cp)
        return cp

    def peer_chip(i):
        return ((lax.rem(chip + i, CHIPS)) * 2 + core, t)

    loads = []
    for c in range(CHUNKS):
        cp = pltpu.make_async_copy(
            raw.at[:, :, pl.ds(c * CHUNK, CHUNK)], y_buf.at[c, pl.ds(HALO, ROWS)], loc_sem.at[c]
        )
        cp.start()
        loads.append(cp)
    foot_load = pltpu.make_async_copy(foot, ff.at[t], loc_sem.at[CHUNKS])
    foot_load.start()
    trace_load = pltpu.make_async_copy(traces, tf.at[chip, core], loc_sem.at[CHUNKS + 1])
    trace_load.start()

    halo_far = (lax.rem(p + NPIX + 2 * core - 1, NPIX), t)
    partners = [sibling, halo_far, across, up, down] + [peer_chip(i) for i in range(1, CHIPS)]
    bar = pltpu.get_barrier_semaphore()
    for dev in partners:
        pl.semaphore_signal(bar, inc=1, device_id=dev, device_id_type=MESH)

    @pl.when(p == 0)
    def _():
        for c in range(CHUNKS):
            y_buf[c, pl.ds(0, HALO)] = jnp.zeros((HALO, COLS, CHUNK), F32)

    @pl.when(p == NPIX - 1)
    def _():
        for c in range(CHUNKS):
            y_buf[c, pl.ds(HALO + ROWS, HALO)] = jnp.zeros((HALO, COLS, CHUNK), F32)

    pl.semaphore_wait(bar, len(partners))

    def halo_down(c):
        return remote(
            raw.at[pl.ds(ROWS - HALO, HALO), :, pl.ds(c * CHUNK, CHUNK)],
            y_buf.at[c, pl.ds(0, HALO)], halo_s.at[0, c], halo_r.at[0, c],
            (lax.rem(p + 1, NPIX), t),
        )

    def halo_up(c):
        return remote(
            raw.at[pl.ds(0, HALO), :, pl.ds(c * CHUNK, CHUNK)],
            y_buf.at[c, pl.ds(HALO + ROWS, HALO)], halo_s.at[1, c], halo_r.at[1, c],
            (lax.rem(p + NPIX - 1, NPIX), t),
        )

    def halo_start(c):
        @pl.when(p < NPIX - 1)
        def _():
            halo_down(c).start()

        @pl.when(p > 0)
        def _():
            halo_up(c).start()

    def halo_wait(c):
        @pl.when(p > 0)
        def _():
            halo_down(c).wait_recv()

        @pl.when(p < NPIX - 1)
        def _():
            halo_up(c).wait_recv()

    def halo_wait_send(c):
        @pl.when(p < NPIX - 1)
        def _():
            halo_down(c).wait_send()

        @pl.when(p > 0)
        def _():
            halo_up(c).wait_send()

    def fblock(j, dz):
        col = xl if j == 1 else 1 - xl
        return col * NZ + lax.rem(z + dz + 2 * NZ, NZ)

    def foot_send(s, j):
        cps = []
        for d in range(2):
            if s == 3 and d == j:
                continue
            sign = -1 if d == 0 else 1
            b = fblock(j, sign * s)
            src = foot if (s == 0 and j == 1) else ff.at[b]
            cps.append(send(src, ff.at[b], fr_s.at[d, s, j], fr_r.at[d, s, j], up if d == 0 else down))
        return cps

    def wait_all(cps):
        for cp in cps:
            cp.wait_recv()

    def gather_chips(src, dst, slot):
        cps = []
        for i in range(1, CHIPS):
            cps.append(send(src, dst, chip_s.at[slot, i], chip_r.at[slot, i], peer_chip(i)))
        return cps

    def rows(c, s, lo, hi):
        src = jnp.where(lax.rem(s, 2) == 1, c, CHUNKS)
        dst = jnp.where(lax.rem(s, 2) == 1, CHUNKS, c)
        col = lax.broadcasted_iota(jnp.int32, (COLS, CHUNK), 0)
        c0 = y_buf[src, lo] - y_buf[src, lo - 1]
        fd_buf[...] = c0 / flux_den(c0)

        def row(r, carry):
            u = y_buf[src, r]
            cd = y_buf[src, r + 1] - u
            ur = jnp.where(col == COLS - 1, 0.0, pltpu.roll(u, COLS - 1, 0))
            cr = ur - u
            dd = flux_den(cd)
            dr = flux_den(cr)
            inv = 1.0 / (dd * dr)
            fdn = cd * (dr * inv)
            frt = cr * (dd * inv)
            u0 = u[0:8]
            edge = u0 / flux_den(u0)
            edge = jnp.concatenate([edge, frt[8:]], axis=0)
            fl = jnp.where(col == 0, edge, pltpu.roll(frt, 1, 0))
            total = (fdn - fd_buf[...]) + (frt - fl)
            fd_buf[...] = fdn
            new = u + STEP * total
            outside = ((p == 0) & (r < HALO)) | ((p == NPIX - 1) & (r >= HALO + ROWS))
            y_buf[dst, r] = jnp.where(outside, 0.0, new)
            return carry

        lax.fori_loop(lo, hi, row, 0)

    def halves(c):
        def body(r, carry):
            hi, lo = split(y_buf[c, HALO + r])
            ph[c, r] = hi
            plo[c, r] = lo
            return carry

        lax.fori_loop(0, ROWS, body, 0)

    def diffuse(c):
        def substep(s, carry):
            rows(c, s, s, EXT - s)
            return carry

        lax.fori_loop(1, HALO + 1, substep, 0)
        halves(c)

    def diffuse_inner(c):
        def substep(s, carry):
            rows(c, s, HALO + s, HALO + ROWS - s)
            return carry

        lax.fori_loop(1, HALO, substep, 0)

    def diffuse_outer(c):
        def substep(k, carry):
            s = 1 + k // 2
            lo = jnp.where(lax.rem(k, 2) == 0, s, EXT - HALO - s)
            rows(c, s, lo, lo + HALO)
            return carry

        lax.fori_loop(0, 2 * HALO, substep, 0)
        halves(c)

    def flip(c):
        def body(r, carry):
            hi, lo = split(y_buf[c, HALO + r].T)
            pth[r, c * CHUNK : (c + 1) * CHUNK] = hi
            ptl[r, c * CHUNK : (c + 1) * CHUNK] = lo
            return carry

        lax.fori_loop(0, ROWS, body, 0)

    def numerator(c):
        def body(r, acc):
            return acc + dot3(fh8[r], fl8[r], ph[c, r], plo[c, r], 0)

        part = lax.fori_loop(0, ROWS, body, jnp.zeros((RANK, CHUNK), F32), unroll=True)
        np_buf[c] = part.reshape(CHIPS, 2, BLK, CHUNK)

    def rs_core(c):
        return send(np_buf.at[c, :, 1 - core], cr_buf.at[c], core_s.at[c], core_r.at[c], sibling)

    def rs_chips(c, cp):
        cp.wait_recv()
        cr_buf[c] = cr_buf[c] + np_buf[c, :, core]
        cps = []
        for i in range(1, CHIPS):
            cps.append(
                send(
                    cr_buf.at[c, lax.rem(chip + i, CHIPS)], lc_buf.at[c, i],
                    chip_s.at[c, i], chip_r.at[c, i], peer_chip(i),
                )
            )
        return cps

    def ag_chips(c, cps):
        wait_all(cps)
        num = cr_buf[c, chip]
        for i in range(1, CHIPS):
            num = num + lc_buf[c, i]
        new = num * scale_buf[:, c * CHUNK : (c + 1) * CHUNK]
        trace_out[:, c * CHUNK : (c + 1) * CHUNK] = new
        mine = nf.at[chip, core, :, pl.ds(c * CHUNK, CHUNK)]
        mine[...] = new
        return gather_chips(mine, mine, CHUNKS + c)

    def ag_core(c, cps):
        wait_all(cps)
        mine = nf.at[:, core, :, pl.ds(c * CHUNK, CHUNK)]
        return send(mine, mine, core_s.at[CHUNKS + c], core_r.at[CHUNKS + c], sibling)

    def foot_update(c, n, cps):
        wait_all(cps)
        lo, hi = c * CHUNK, (c + n) * CHUNK
        nh, nl = split(nf[:, :, :, lo:hi].reshape(RANK, n * CHUNK))
        first = c == 0

        def put(where, val):
            val = val.reshape(NB, BLK, RANK)
            fn[:, :, where] = val if first else fn[:, :, where] + val

        put(pl.ds(LOCAL, RANK), dot3(nh, nl, nh, nl, 1))

        def body(r, carry):
            put(
                pl.ds(pl.multiple_of(r * COLS, COLS), COLS),
                dot3(nh, nl, pth[r, lo:hi], ptl[r, lo:hi], 0),
            )
            return carry

        lax.fori_loop(0, ROWS, body, 0, unroll=True)

    fx = send(foot, ff.at[t], fx_s.at[0], fx_r.at[0], across)
    own0 = foot_send(0, 1)
    halo_start(0)
    halo_start(1)
    halo_start(2)
    halo_start(3)
    fx.wait_recv()
    oth0 = foot_send(0, 0)
    wait_all(own0)
    own1 = foot_send(1, 1)
    wait_all(oth0)
    oth1 = foot_send(1, 0)
    for cp in loads:
        cp.wait()
    halo_wait(0)
    wait_all(own1)
    own2 = foot_send(2, 1)
    wait_all(oth1)
    oth2 = foot_send(2, 0)
    diffuse(0)
    stores = []

    def store(c):
        cp = pltpu.make_async_copy(
            y_buf.at[c, pl.ds(HALO, ROWS)], den_out.at[:, :, pl.ds(c * CHUNK, CHUNK)], out_sem.at[c]
        )
        cp.start()
        stores.append(cp)

    store(0)
    wait_all(own2)
    own3 = foot_send(3, 1)
    wait_all(oth2)
    oth3 = foot_send(3, 0)
    foot_load.wait()
    trace_load.wait()
    halo_wait(1)
    diffuse(1)
    store(1)
    wait_all(own3)
    wait_all(oth3)

    def split_foot(r, carry):
        hi, lo = split(ff[:, :, pl.ds(pl.multiple_of(r * COLS, COLS), COLS)].reshape(RANK, COLS))
        fh8[r] = hi
        fl8[r] = lo
        return carry

    lax.fori_loop(0, ROWS, split_foot, 0)

    def gram_body(r, acc):
        return acc + dot3(fh8[r], fl8[r], fh8[r], fl8[r], 1)

    gp[...] = lax.fori_loop(0, ROWS, gram_body, jnp.zeros((RANK, RANK), F32), unroll=True).reshape(CHIPS, 2, BLK, RANK)
    gslot = 2 * CHUNKS + 1
    g_core = send(gp.at[:, 1 - core], gcr, core_s.at[gslot], core_r.at[gslot], sibling)
    numerator(0)
    rs0 = rs_core(0)
    numerator(1)
    rs1 = rs_core(1)
    halo_wait(2)
    diffuse(2)
    store(2)
    numerator(2)
    rs2 = rs_core(2)
    diffuse_inner(3)
    flip(0)
    flip(1)
    flip(2)
    halo_wait(3)

    tr = gather_chips(traces, tf.at[chip, core], 2 * CHUNKS)
    g_core.wait_recv()
    gcr[...] = gcr[...] + gp[:, core]
    g_chips = []
    for i in range(1, CHIPS):
        g_chips.append(
            send(gcr.at[lax.rem(chip + i, CHIPS)], gl.at[i], chip_s.at[gslot, i], chip_r.at[gslot, i], peer_chip(i))
        )
    rs0 = rs_chips(0, rs0)
    rs1 = rs_chips(1, rs1)
    rs2 = rs_chips(2, rs2)
    diffuse_outer(3)
    store(3)
    numerator(3)
    rs3 = rs_core(3)
    wait_all(tr)
    tr_core = send(tf.at[:, core], tf.at[:, core], core_s.at[2 * CHUNKS], core_r.at[2 * CHUNKS], sibling)
    wait_all(g_chips)
    gram = gcr[chip]
    for i in range(1, CHIPS):
        gram = gram + gl[i]
    rs3 = rs_chips(3, rs3)
    flip(3)
    tr_core.wait_recv()
    gh, gl_ = split(gram)
    th, tl = split(tf[...].reshape(RANK, FRAMES))
    scale_buf[...] = tf[chip, core] / dot3(gh, gl_, th, tl, 0)
    ag0 = ag_chips(0, rs0)
    ag1 = ag_chips(1, rs1)
    ag2 = ag_chips(2, rs2)
    ag3 = ag_chips(3, rs3)
    ag0 = ag_core(0, ag0)
    ag1 = ag_core(1, ag1)
    ag2 = ag_core(2, ag2)
    foot_update(0, 2, (ag0, ag1))
    foot_update(2, 1, (ag2,))
    ag3 = ag_core(3, ag3)
    foot_update(3, 1, (ag3,))

    def ring_send(s, j, got):
        cps = []
        for d in range(2):
            if s == 0 and d == j:
                continue
            land = lu if d == 0 else ld
            b = fblock(j, (NZ // 2 - s) * (1 if d == 0 else -1))
            if d in got:
                land[s - 1, j] = land[s - 1, j] + fn[b]
                src = land.at[s - 1, j]
            else:
                src = fn.at[b]
            cps.append(send(src, land.at[s, j], ring_s.at[d, s, j], ring_r.at[d, s, j], up if d == 0 else down))
        return cps

    r0 = ring_send(0, 0, ())
    r1 = ring_send(0, 1, ())
    for s in range(1, 4):
        wait_all(r0)
        r0 = ring_send(s, 0, (1,) if s == 1 else (0, 1))
        wait_all(r1)
        r1 = ring_send(s, 1, (0,) if s == 1 else (0, 1))
    wait_all(r0)
    bo = fblock(0, 0)
    lu[3, 0] = (lu[3, 0] + ld[3, 0]) + fn[bo]
    rx = send(lu.at[3, 0], lx, rx_s.at[0], rx_r.at[0], across)
    wait_all(r1)
    lu[3, 1] = (lu[3, 1] + ld[3, 1]) + fn[fblock(1, 0)]
    rx.wait_recv()
    kh, kl = split(lu[3, 1, :, pl.ds(LOCAL, RANK)] + lx[:, pl.ds(LOCAL, RANK)])

    def final(r, carry):
        w = pl.ds(pl.multiple_of(r * COLS, COLS), COLS)
        den = dot3(kh, kl, fh8[r], fl8[r], 0)
        foot_out[:, w] = ff[t, :, w] * (lu[3, 1, :, w] + lx[:, w]) / den
        return carry

    lax.fori_loop(0, ROWS, final, 0, unroll=True)

    for cp in pending:
        cp.wait_send()
    for c in range(CHUNKS):
        halo_wait_send(c)
    for cp in stores:
        cp.wait()


def body(raw_movie, footprints, traces):
    dma = pltpu.SemaphoreType.DMA
    vm = pltpu.VMEM
    hbm = pl.BlockSpec(memory_space=pltpu.MemorySpace.HBM)
    inv = pl.BlockSpec(memory_space=pltpu.MemorySpace.VMEM)
    return pl.pallas_call(
        kernel,
        out_shape=(
            jax.ShapeDtypeStruct(raw_movie.shape, F32),
            jax.ShapeDtypeStruct(footprints.shape, F32),
            jax.ShapeDtypeStruct(traces.shape, F32),
        ),
        in_specs=[hbm, hbm, hbm],
        out_specs=(hbm, inv, inv),
        scratch_shapes=[
            vm((CHUNKS + 1, EXT, COLS, CHUNK), F32),
            vm((COLS, CHUNK), F32),
            vm((CHUNKS, ROWS, COLS, CHUNK), BF16),
            vm((CHUNKS, ROWS, COLS, CHUNK), BF16),
            vm((NB, BLK, LOCAL), F32),
            vm((ROWS, RANK, COLS), BF16),
            vm((ROWS, RANK, COLS), BF16),
            vm((NB, BLK, WIDE), F32),
            vm((4, 2, BLK, WIDE), F32),
            vm((4, 2, BLK, WIDE), F32),
            vm((BLK, WIDE), F32),
            vm((CHIPS, 2, BLK, RANK), F32),
            vm((CHIPS, BLK, RANK), F32),
            vm((CHIPS, BLK, RANK), F32),
            vm((CHIPS, 2, BLK, FRAMES), F32),
            vm((BLK, FRAMES), F32),
            vm((CHUNKS, CHIPS, 2, BLK, CHUNK), F32),
            vm((CHUNKS, CHIPS, BLK, CHUNK), F32),
            vm((CHUNKS, CHIPS, BLK, CHUNK), F32),
            vm((CHIPS, 2, BLK, FRAMES), F32),
            vm((ROWS, FRAMES, COLS), BF16),
            vm((ROWS, FRAMES, COLS), BF16),
            dma((CHUNKS + 2,)),
            dma((CHUNKS,)),
            dma((2, CHUNKS)),
            dma((2, CHUNKS)),
            dma((1,)),
            dma((1,)),
            dma((2, 4, 2)),
            dma((2, 4, 2)),
            dma((2, 4, 2)),
            dma((2, 4, 2)),
            dma((1,)),
            dma((1,)),
            dma((2 * CHUNKS + 2,)),
            dma((2 * CHUNKS + 2,)),
            dma((2 * CHUNKS + 2, CHIPS)),
            dma((2 * CHUNKS + 2, CHIPS)),
        ],
        compiler_params=pltpu.CompilerParams(
            collective_id=0, has_side_effects=True, vmem_limit_bytes=48 * 1024 * 1024
        ),
        cost_estimate=pl.CostEstimate(flops=4 * 10**9, bytes_accessed=16 * 2**20, transcendentals=0),
    )(raw_movie, footprints, traces)


def solution(mesh):
    placed = (P("pix", None, "tm"), P("tm", "pix"), P("pix", "tm"))
    return jax.shard_map(body, mesh=mesh, in_specs=placed, out_specs=placed, check_vma=False)
```

```python
import jax
import jax.numpy as jnp
from jax import lax
from jax.experimental import pallas as pl
from jax.experimental.pallas import tpu as pltpu
from jax.sharding import PartitionSpec as P

F32 = jnp.float32
BF16 = jnp.bfloat16
MESH = pl.DeviceIdType.MESH
HALO = 4
ROWS = 8
EXT = ROWS + 2 * HALO
COLS = 256
FRAMES = 512
CHUNK = 128
CHUNKS = FRAMES // CHUNK
RANK = 256
BLK = 16
NB = RANK // BLK
CHIPS = 8
NPIX = 16
NZ = 8
LOCAL = ROWS * COLS
WIDE = LOCAL + RANK
STEP = 0.24
PART = 1024
REST = WIDE - PART


def split(x):
    hi = x.astype(BF16)
    return hi, (x - hi.astype(F32)).astype(BF16)


def dot3(ah, al, bh, bl, rhs_dim):
    dims = (((1,), (rhs_dim,)), ((), ()))

    def one(a, b):
        return lax.dot_general(a, b, dims, preferred_element_type=F32)

    return one(ah, bh) + (one(al, bh) + one(ah, bl))


def flux_den(c):
    return 1.0 + 4.0 * (c * c)


def kernel(
    raw, foot, traces, den_out, foot_out, trace_out,
    y_buf, fd_buf, ph, plo, ff, fh8, fl8, fn, lu, ld, lx, gp, gcr, gl, tf, scale_buf,
    np_buf, cr_buf, lc_buf, nf, pth, ptl, xb, lub, ldb,
    loc_sem, out_sem, halo_s, halo_r, fx_s, fx_r, fr_s, fr_r, ring_s, ring_r, rx_s, rx_r,
    core_s, core_r, chip_s, chip_r, rest_s, rest_r,
):
    p = lax.axis_index("pix")
    t = lax.axis_index("tm")
    chip = p // 2
    core = p % 2
    xl = t // NZ
    z = t % NZ
    up = (p, xl * NZ + (z + 1) % NZ)
    down = (p, xl * NZ + (z + NZ - 1) % NZ)
    across = (p, (1 - xl) * NZ + z)
    sibling = (chip * 2 + (1 - core), t)
    pending = []

    def remote(src, dst, ssem, rsem, dev):
        return pltpu.make_async_remote_copy(
            src_ref=src, dst_ref=dst, send_sem=ssem, recv_sem=rsem, device_id=dev, device_id_type=MESH
        )

    def send(*args):
        cp = remote(*args)
        cp.start()
        pending.append(cp)
        return cp

    def peer_chip(i):
        return ((lax.rem(chip + i, CHIPS)) * 2 + core, t)

    loads = []
    for c in range(CHUNKS):
        cp = pltpu.make_async_copy(
            raw.at[:, :, pl.ds(c * CHUNK, CHUNK)], y_buf.at[c, pl.ds(HALO, ROWS)], loc_sem.at[c]
        )
        cp.start()
        loads.append(cp)
    foot_load = pltpu.make_async_copy(foot, ff.at[t], loc_sem.at[CHUNKS])
    foot_load.start()
    trace_load = pltpu.make_async_copy(traces, tf.at[chip, core], loc_sem.at[CHUNKS + 1])
    trace_load.start()

    halo_far = (lax.rem(p + NPIX + 2 * core - 1, NPIX), t)
    partners = [sibling, halo_far, across, up, down] + [peer_chip(i) for i in range(1, CHIPS)]
    bar = pltpu.get_barrier_semaphore()
    for dev in partners:
        pl.semaphore_signal(bar, inc=1, device_id=dev, device_id_type=MESH)

    @pl.when(p == 0)
    def _():
        for c in range(CHUNKS):
            y_buf[c, pl.ds(0, HALO)] = jnp.zeros((HALO, COLS, CHUNK), F32)

    @pl.when(p == NPIX - 1)
    def _():
        for c in range(CHUNKS):
            y_buf[c, pl.ds(HALO + ROWS, HALO)] = jnp.zeros((HALO, COLS, CHUNK), F32)

    pl.semaphore_wait(bar, len(partners))

    def halo_down(c):
        return remote(
            raw.at[pl.ds(ROWS - HALO, HALO), :, pl.ds(c * CHUNK, CHUNK)],
            y_buf.at[c, pl.ds(0, HALO)], halo_s.at[0, c], halo_r.at[0, c],
            (lax.rem(p + 1, NPIX), t),
        )

    def halo_up(c):
        return remote(
            raw.at[pl.ds(0, HALO), :, pl.ds(c * CHUNK, CHUNK)],
            y_buf.at[c, pl.ds(HALO + ROWS, HALO)], halo_s.at[1, c], halo_r.at[1, c],
            (lax.rem(p + NPIX - 1, NPIX), t),
        )

    def halo_start(c):
        @pl.when(p < NPIX - 1)
        def _():
            halo_down(c).start()

        @pl.when(p > 0)
        def _():
            halo_up(c).start()

    def halo_wait(c):
        @pl.when(p > 0)
        def _():
            halo_down(c).wait_recv()

        @pl.when(p < NPIX - 1)
        def _():
            halo_up(c).wait_recv()

    def halo_wait_send(c):
        @pl.when(p < NPIX - 1)
        def _():
            halo_down(c).wait_send()

        @pl.when(p > 0)
        def _():
            halo_up(c).wait_send()

    def fblock(j, dz):
        col = xl if j == 1 else 1 - xl
        return col * NZ + lax.rem(z + dz + 2 * NZ, NZ)

    def foot_send(s, j):
        cps = []
        for d in range(2):
            if s == 3 and d == j:
                continue
            sign = -1 if d == 0 else 1
            b = fblock(j, sign * s)
            src = foot if (s == 0 and j == 1) else ff.at[b]
            cps.append(send(src, ff.at[b], fr_s.at[d, s, j], fr_r.at[d, s, j], up if d == 0 else down))
        return cps

    def wait_all(cps):
        for cp in cps:
            cp.wait_recv()

    def gather_chips(src, dst, slot):
        cps = []
        for i in range(1, CHIPS):
            cps.append(send(src, dst, chip_s.at[slot, i], chip_r.at[slot, i], peer_chip(i)))
        return cps

    def rows(c, s, lo, hi):
        src = jnp.where(lax.rem(s, 2) == 1, c, CHUNKS)
        dst = jnp.where(lax.rem(s, 2) == 1, CHUNKS, c)
        col = lax.broadcasted_iota(jnp.int32, (COLS, CHUNK), 0)
        c0 = y_buf[src, lo] - y_buf[src, lo - 1]
        fd_buf[...] = c0 / flux_den(c0)

        def row(r, carry):
            u = y_buf[src, r]
            cd = y_buf[src, r + 1] - u
            ur = jnp.where(col == COLS - 1, 0.0, pltpu.roll(u, COLS - 1, 0))
            cr = ur - u
            dd = flux_den(cd)
            dr = flux_den(cr)
            inv = 1.0 / (dd * dr)
            fdn = cd * (dr * inv)
            frt = cr * (dd * inv)
            u0 = u[0:8]
            edge = u0 / flux_den(u0)
            edge = jnp.concatenate([edge, frt[8:]], axis=0)
            fl = jnp.where(col == 0, edge, pltpu.roll(frt, 1, 0))
            total = (fdn - fd_buf[...]) + (frt - fl)
            fd_buf[...] = fdn
            new = u + STEP * total
            outside = ((p == 0) & (r < HALO)) | ((p == NPIX - 1) & (r >= HALO + ROWS))
            y_buf[dst, r] = jnp.where(outside, 0.0, new)
            return carry

        lax.fori_loop(lo, hi, row, 0)

    def halves(c):
        def body(r, carry):
            hi, lo = split(y_buf[c, HALO + r])
            ph[c, r] = hi
            plo[c, r] = lo
            return carry

        lax.fori_loop(0, ROWS, body, 0)

    def diffuse(c):
        def substep(s, carry):
            rows(c, s, s, EXT - s)
            return carry

        lax.fori_loop(1, HALO + 1, substep, 0)
        halves(c)

    def diffuse_inner(c):
        def substep(s, carry):
            rows(c, s, HALO + s, HALO + ROWS - s)
            return carry

        lax.fori_loop(1, HALO, substep, 0)

    def diffuse_outer(c):
        def substep(k, carry):
            s = 1 + k // 2
            lo = jnp.where(lax.rem(k, 2) == 0, s, EXT - HALO - s)
            rows(c, s, lo, lo + HALO)
            return carry

        lax.fori_loop(0, 2 * HALO, substep, 0)
        halves(c)

    def flip(c):
        def body(r, carry):
            hi, lo = split(y_buf[c, HALO + r].T)
            pth[r, c * CHUNK : (c + 1) * CHUNK] = hi
            ptl[r, c * CHUNK : (c + 1) * CHUNK] = lo
            return carry

        lax.fori_loop(0, ROWS, body, 0)

    def numerator(c):
        def body(r, acc):
            return acc + dot3(fh8[r], fl8[r], ph[c, r], plo[c, r], 0)

        part = lax.fori_loop(0, ROWS, body, jnp.zeros((RANK, CHUNK), F32), unroll=True)
        np_buf[c] = part.reshape(CHIPS, 2, BLK, CHUNK)

    def rs_core(c):
        return send(np_buf.at[c, :, 1 - core], cr_buf.at[c], core_s.at[c], core_r.at[c], sibling)

    def rs_chips(c, cp):
        cp.wait_recv()
        cr_buf[c] = cr_buf[c] + np_buf[c, :, core]
        cps = []
        for i in range(1, CHIPS):
            cps.append(
                send(
                    cr_buf.at[c, lax.rem(chip + i, CHIPS)], lc_buf.at[c, i],
                    chip_s.at[c, i], chip_r.at[c, i], peer_chip(i),
                )
            )
        return cps

    def ag_chips(c, cps):
        wait_all(cps)
        num = cr_buf[c, chip]
        for i in range(1, CHIPS):
            num = num + lc_buf[c, i]
        new = num * scale_buf[:, c * CHUNK : (c + 1) * CHUNK]
        trace_out[:, c * CHUNK : (c + 1) * CHUNK] = new
        mine = nf.at[chip, core, :, pl.ds(c * CHUNK, CHUNK)]
        mine[...] = new
        return gather_chips(mine, mine, CHUNKS + c)

    def ag_core(c, cps):
        wait_all(cps)
        mine = nf.at[:, core, :, pl.ds(c * CHUNK, CHUNK)]
        return send(mine, mine, core_s.at[CHUNKS + c], core_r.at[CHUNKS + c], sibling)

    def foot_update(c, n, cps):
        wait_all(cps)
        lo, hi = c * CHUNK, (c + n) * CHUNK
        nh, nl = split(nf[:, :, :, lo:hi].reshape(RANK, n * CHUNK))
        first = c == 0

        def put(where, val):
            val = val.reshape(NB, BLK, RANK)
            fn[:, :, where] = val if first else fn[:, :, where] + val

        put(pl.ds(LOCAL, RANK), dot3(nh, nl, nh, nl, 1))

        def body(r, carry):
            put(
                pl.ds(pl.multiple_of(r * COLS, COLS), COLS),
                dot3(nh, nl, pth[r, lo:hi], ptl[r, lo:hi], 0),
            )
            return carry

        lax.fori_loop(0, ROWS, body, 0, unroll=True)

    fx = send(foot, ff.at[t], fx_s.at[0], fx_r.at[0], across)
    own0 = foot_send(0, 1)
    halo_start(0)
    halo_start(1)
    halo_start(2)
    halo_start(3)
    fx.wait_recv()
    oth0 = foot_send(0, 0)
    wait_all(own0)
    own1 = foot_send(1, 1)
    wait_all(oth0)
    oth1 = foot_send(1, 0)
    for cp in loads:
        cp.wait()
    halo_wait(0)
    wait_all(own1)
    own2 = foot_send(2, 1)
    wait_all(oth1)
    oth2 = foot_send(2, 0)
    diffuse(0)
    stores = []

    def store(c):
        cp = pltpu.make_async_copy(
            y_buf.at[c, pl.ds(HALO, ROWS)], den_out.at[:, :, pl.ds(c * CHUNK, CHUNK)], out_sem.at[c]
        )
        cp.start()
        stores.append(cp)

    store(0)
    wait_all(own2)
    own3 = foot_send(3, 1)
    wait_all(oth2)
    oth3 = foot_send(3, 0)
    foot_load.wait()
    trace_load.wait()
    halo_wait(1)
    diffuse(1)
    store(1)
    wait_all(own3)
    wait_all(oth3)

    def split_foot(r, carry):
        hi, lo = split(ff[:, :, pl.ds(pl.multiple_of(r * COLS, COLS), COLS)].reshape(RANK, COLS))
        fh8[r] = hi
        fl8[r] = lo
        return carry

    lax.fori_loop(0, ROWS, split_foot, 0)

    def gram_body(r, acc):
        return acc + dot3(fh8[r], fl8[r], fh8[r], fl8[r], 1)

    gp[...] = lax.fori_loop(0, ROWS, gram_body, jnp.zeros((RANK, RANK), F32), unroll=True).reshape(CHIPS, 2, BLK, RANK)
    gslot = 2 * CHUNKS + 1
    g_core = send(gp.at[:, 1 - core], gcr, core_s.at[gslot], core_r.at[gslot], sibling)
    numerator(0)
    rs0 = rs_core(0)
    numerator(1)
    rs1 = rs_core(1)
    halo_wait(2)
    diffuse(2)
    store(2)
    numerator(2)
    rs2 = rs_core(2)
    diffuse_inner(3)
    flip(0)
    flip(1)
    flip(2)
    halo_wait(3)

    tr = gather_chips(traces, tf.at[chip, core], 2 * CHUNKS)
    g_core.wait_recv()
    gcr[...] = gcr[...] + gp[:, core]
    g_chips = []
    for i in range(1, CHIPS):
        g_chips.append(
            send(gcr.at[lax.rem(chip + i, CHIPS)], gl.at[i], chip_s.at[gslot, i], chip_r.at[gslot, i], peer_chip(i))
        )
    rs0 = rs_chips(0, rs0)
    rs1 = rs_chips(1, rs1)
    rs2 = rs_chips(2, rs2)
    diffuse_outer(3)
    store(3)
    numerator(3)
    rs3 = rs_core(3)
    wait_all(tr)
    tr_core = send(tf.at[:, core], tf.at[:, core], core_s.at[2 * CHUNKS], core_r.at[2 * CHUNKS], sibling)
    wait_all(g_chips)
    gram = gcr[chip]
    for i in range(1, CHIPS):
        gram = gram + gl[i]
    rs3 = rs_chips(3, rs3)
    flip(3)
    tr_core.wait_recv()
    gh, gl_ = split(gram)
    th, tl = split(tf[...].reshape(RANK, FRAMES))
    scale_buf[...] = tf[chip, core] / dot3(gh, gl_, th, tl, 0)
    ag0 = ag_chips(0, rs0)
    ag1 = ag_chips(1, rs1)
    ag2 = ag_chips(2, rs2)
    ag3 = ag_chips(3, rs3)
    ag0 = ag_core(0, ag0)
    ag1 = ag_core(1, ag1)
    ag2 = ag_core(2, ag2)
    foot_update(0, 2, (ag0, ag1))
    foot_update(2, 1, (ag2,))
    ag3 = ag_core(3, ag3)
    foot_update(3, 1, (ag3,))

    def low(ref, b):
        return ref.at[b, :, pl.ds(0, PART)]

    def ring_send(s, j, got):
        cps = []
        for d in range(2):
            if s == 0 and d == j:
                continue
            land = lu if d == 0 else ld
            b = fblock(j, (NZ // 2 - s) * (1 if d == 0 else -1))
            if d in got:
                land[s - 1, j] = land[s - 1, j] + fn[b, :, :PART]
                src = land.at[s - 1, j]
            else:
                src = low(fn, b)
            cps.append(send(src, land.at[s, j], ring_s.at[d, s, j], ring_r.at[d, s, j], up if d == 0 else down))
        return cps

    cross = {}
    for dz in (4, 3, -3, 2, -2, 1, -1, 0):
        k = dz % NZ
        cross[dz] = send(
            fn.at[fblock(0, dz), :, pl.ds(PART, REST)], xb.at[k], rx_s.at[k], rx_r.at[k], across
        )

    def take(dz):
        cross[dz].wait_recv()
        k = dz % NZ
        xb[k] = xb[k] + fn[fblock(1, dz), :, PART:]

    def rest_send(s, cps):
        if s == 0:
            take(4)
        else:
            take(4 - s)
            take(s - 4)
            wait_all(cps)
        out = []
        for d in range(2):
            land = lub if d == 0 else ldb
            k = ((4 - s) * (1 if d == 0 else -1)) % NZ
            w = pl.ds(d * (REST // 2), REST // 2) if s <= 1 else pl.ds(0, REST)
            if s > 0:
                xb[k, :, w] = xb[k, :, w] + land[s - 1, :, w]
            w = w if s == 0 else pl.ds(0, REST)
            out.append(
                send(xb.at[k, :, w], land.at[s, :, w], rest_s.at[d, s], rest_r.at[d, s], up if d == 0 else down)
            )
        return out

    r0 = ring_send(0, 0, ())
    r1 = ring_send(0, 1, ())
    rb = rest_send(0, ())
    for s in range(1, 4):
        wait_all(r0)
        r0 = ring_send(s, 0, (1,) if s == 1 else (0, 1))
        wait_all(r1)
        r1 = ring_send(s, 1, (0,) if s == 1 else (0, 1))
        rb = rest_send(s, rb)
    wait_all(r0)
    lu[3, 0] = (lu[3, 0] + ld[3, 0]) + fn[fblock(0, 0), :, :PART]
    rx = send(lu.at[3, 0], lx, rx_s.at[NZ], rx_r.at[NZ], across)
    wait_all(r1)
    lu[3, 1] = (lu[3, 1] + ld[3, 1]) + fn[fblock(1, 0), :, :PART]
    take(0)
    wait_all(rb)
    xb[0] = xb[0] + (lub[3] + ldb[3])
    kh, kl = split(xb[0, :, LOCAL - PART :])

    def final(r):
        w = slice(r * COLS, (r + 1) * COLS)
        den = dot3(kh, kl, fh8[r], fl8[r], 0)
        if w.start >= PART:
            num = xb[0, :, w.start - PART : w.stop - PART]
        else:
            num = lu[3, 1, :, w] + lx[:, w]
        foot_out[:, w] = ff[t, :, w] * num / den

    for r in range(PART // COLS, ROWS):
        final(r)
    rx.wait_recv()
    for r in range(PART // COLS):
        final(r)

    for cp in pending:
        cp.wait_send()
    for c in range(CHUNKS):
        halo_wait_send(c)
    for cp in stores:
        cp.wait()


def move_out(den, foot, trace, den_hbm, foot_hbm, trace_hbm, sems):
    cps = [pltpu.make_async_copy(den.at[r], den_hbm.at[r], sems.at[r]) for r in range(ROWS)]
    cps.append(pltpu.make_async_copy(foot, foot_hbm, sems.at[ROWS]))
    cps.append(pltpu.make_async_copy(trace, trace_hbm, sems.at[ROWS + 1]))
    for cp in cps:
        cp.start()
    for cp in cps:
        cp.wait()


def stay(x):
    return pltpu.with_memory_space_constraint(x, pltpu.MemorySpace.HBM)


def body(raw_movie, footprints, traces):
    dma = pltpu.SemaphoreType.DMA
    vm = pltpu.VMEM
    hbm = pl.BlockSpec(memory_space=pltpu.MemorySpace.HBM)
    inv = pl.BlockSpec(memory_space=pltpu.MemorySpace.VMEM)
    outs = pl.pallas_call(
        kernel,
        out_shape=(
            jax.ShapeDtypeStruct(raw_movie.shape, F32),
            jax.ShapeDtypeStruct(footprints.shape, F32),
            jax.ShapeDtypeStruct(traces.shape, F32),
        ),
        in_specs=[hbm, hbm, hbm],
        out_specs=(inv, inv, inv),
        scratch_shapes=[
            vm((CHUNKS + 1, EXT, COLS, CHUNK), F32),
            vm((COLS, CHUNK), F32),
            vm((CHUNKS, ROWS, COLS, CHUNK), BF16),
            vm((CHUNKS, ROWS, COLS, CHUNK), BF16),
            vm((NB, BLK, LOCAL), F32),
            vm((ROWS, RANK, COLS), BF16),
            vm((ROWS, RANK, COLS), BF16),
            vm((NB, BLK, WIDE), F32),
            vm((4, 2, BLK, PART), F32),
            vm((4, 2, BLK, PART), F32),
            vm((BLK, PART), F32),
            vm((CHIPS, 2, BLK, RANK), F32),
            vm((CHIPS, BLK, RANK), F32),
            vm((CHIPS, BLK, RANK), F32),
            vm((CHIPS, 2, BLK, FRAMES), F32),
            vm((BLK, FRAMES), F32),
            vm((CHUNKS, CHIPS, 2, BLK, CHUNK), F32),
            vm((CHUNKS, CHIPS, BLK, CHUNK), F32),
            vm((CHUNKS, CHIPS, BLK, CHUNK), F32),
            vm((CHIPS, 2, BLK, FRAMES), F32),
            vm((ROWS, FRAMES, COLS), BF16),
            vm((ROWS, FRAMES, COLS), BF16),
            vm((NZ, BLK, REST), F32),
            vm((4, BLK, REST), F32),
            vm((4, BLK, REST), F32),
            dma((CHUNKS + 2,)),
            dma((CHUNKS,)),
            dma((2, CHUNKS)),
            dma((2, CHUNKS)),
            dma((1,)),
            dma((1,)),
            dma((2, 4, 2)),
            dma((2, 4, 2)),
            dma((2, 4, 2)),
            dma((2, 4, 2)),
            dma((NZ + 1,)),
            dma((NZ + 1,)),
            dma((2 * CHUNKS + 2,)),
            dma((2 * CHUNKS + 2,)),
            dma((2 * CHUNKS + 2, CHIPS)),
            dma((2 * CHUNKS + 2, CHIPS)),
            dma((2, 4)),
            dma((2, 4)),
        ],
        compiler_params=pltpu.CompilerParams(
            collective_id=0, has_side_effects=True, vmem_limit_bytes=48 * 1024 * 1024
        ),
        cost_estimate=pl.CostEstimate(flops=4 * 10**9, bytes_accessed=16 * 2**20, transcendentals=0),
    )(raw_movie, stay(footprints), stay(traces))
    return pl.pallas_call(
        move_out,
        out_shape=tuple(jax.ShapeDtypeStruct(o.shape, F32) for o in outs),
        in_specs=[inv, inv, inv],
        out_specs=(hbm, hbm, hbm),
        scratch_shapes=[dma((ROWS + 2,))],
        compiler_params=pltpu.CompilerParams(vmem_limit_bytes=8 * 1024 * 1024),
    )(*outs)


def solution(mesh):
    placed = (P("pix", None, "tm"), P("tm", "pix"), P("pix", "tm"))
    return jax.shard_map(body, mesh=mesh, in_specs=placed, out_specs=placed, check_vma=False)
```

```python
import jax
import jax.numpy as jnp
from jax import lax
from jax.experimental import pallas as pl
from jax.experimental.pallas import tpu as pltpu
from jax.sharding import PartitionSpec as P

F32 = jnp.float32
BF16 = jnp.bfloat16
MESH = pl.DeviceIdType.MESH
HALO = 4
ROWS = 8
EXT = ROWS + 2 * HALO
COLS = 256
FRAMES = 512
CHUNK = 128
CHUNKS = FRAMES // CHUNK
RANK = 256
BLK = 16
NB = RANK // BLK
CHIPS = 8
NPIX = 16
NZ = 8
LOCAL = ROWS * COLS
WIDE = LOCAL + RANK
STEP = 0.24
PART = 1024
REST = WIDE - PART


def split(x):
    hi = x.astype(BF16)
    return hi, (x - hi.astype(F32)).astype(BF16)


def dot3(ah, al, bh, bl, rhs_dim):
    dims = (((1,), (rhs_dim,)), ((), ()))

    def one(a, b):
        return lax.dot_general(a, b, dims, preferred_element_type=F32)

    return one(ah, bh) + (one(al, bh) + one(ah, bl))


def flux_den(c):
    return 1.0 + 4.0 * (c * c)


def kernel(
    raw, foot, traces, den_out, foot_out, trace_out,
    y_buf, fd_buf, ph, plo, ff, fh8, fl8, fn, lu, ld, lx, gp, gcr, gl, tf, scale_buf,
    np_buf, cr_buf, lc_buf, nf, pth, ptl, xb, lub, ldb,
    loc_sem, out_sem, halo_s, halo_r, fx_s, fx_r, fr_s, fr_r, ring_s, ring_r, rx_s, rx_r,
    core_s, core_r, chip_s, chip_r, rest_s, rest_r,
):
    p = lax.axis_index("pix")
    t = lax.axis_index("tm")
    chip = p // 2
    core = p % 2
    xl = t // NZ
    z = t % NZ
    up = (p, xl * NZ + (z + 1) % NZ)
    down = (p, xl * NZ + (z + NZ - 1) % NZ)
    across = (p, (1 - xl) * NZ + z)
    sibling = (chip * 2 + (1 - core), t)
    pending = []

    def remote(src, dst, ssem, rsem, dev):
        return pltpu.make_async_remote_copy(
            src_ref=src, dst_ref=dst, send_sem=ssem, recv_sem=rsem, device_id=dev, device_id_type=MESH
        )

    def send(*args):
        cp = remote(*args)
        cp.start()
        pending.append(cp)
        return cp

    def peer_chip(i):
        return ((lax.rem(chip + i, CHIPS)) * 2 + core, t)

    loads = []
    for c in range(CHUNKS):
        cp = pltpu.make_async_copy(
            raw.at[:, :, pl.ds(c * CHUNK, CHUNK)], y_buf.at[c, pl.ds(HALO, ROWS)], loc_sem.at[c]
        )
        cp.start()
        loads.append(cp)
    foot_load = pltpu.make_async_copy(foot, ff.at[t], loc_sem.at[CHUNKS])
    foot_load.start()
    trace_load = pltpu.make_async_copy(traces, tf.at[chip, core], loc_sem.at[CHUNKS + 1])
    trace_load.start()

    halo_far = (lax.rem(p + NPIX + 2 * core - 1, NPIX), t)
    partners = [sibling, halo_far, across, up, down] + [peer_chip(i) for i in range(1, CHIPS)]
    bar = pltpu.get_barrier_semaphore()
    for dev in partners:
        pl.semaphore_signal(bar, inc=1, device_id=dev, device_id_type=MESH)

    @pl.when(p == 0)
    def _():
        for c in range(CHUNKS):
            y_buf[c, pl.ds(0, HALO)] = jnp.zeros((HALO, COLS, CHUNK), F32)

    @pl.when(p == NPIX - 1)
    def _():
        for c in range(CHUNKS):
            y_buf[c, pl.ds(HALO + ROWS, HALO)] = jnp.zeros((HALO, COLS, CHUNK), F32)

    pl.semaphore_wait(bar, len(partners))

    def halo_down(c):
        return remote(
            raw.at[pl.ds(ROWS - HALO, HALO), :, pl.ds(c * CHUNK, CHUNK)],
            y_buf.at[c, pl.ds(0, HALO)], halo_s.at[0, c], halo_r.at[0, c],
            (lax.rem(p + 1, NPIX), t),
        )

    def halo_up(c):
        return remote(
            raw.at[pl.ds(0, HALO), :, pl.ds(c * CHUNK, CHUNK)],
            y_buf.at[c, pl.ds(HALO + ROWS, HALO)], halo_s.at[1, c], halo_r.at[1, c],
            (lax.rem(p + NPIX - 1, NPIX), t),
        )

    def halo_start(c):
        @pl.when(p < NPIX - 1)
        def _():
            halo_down(c).start()

        @pl.when(p > 0)
        def _():
            halo_up(c).start()

    def halo_wait(c):
        @pl.when(p > 0)
        def _():
            halo_down(c).wait_recv()

        @pl.when(p < NPIX - 1)
        def _():
            halo_up(c).wait_recv()

    def halo_wait_send(c):
        @pl.when(p < NPIX - 1)
        def _():
            halo_down(c).wait_send()

        @pl.when(p > 0)
        def _():
            halo_up(c).wait_send()

    def fblock(j, dz):
        col = xl if j == 1 else 1 - xl
        return col * NZ + lax.rem(z + dz + 2 * NZ, NZ)

    def foot_send(s, j):
        cps = []
        for d in range(2):
            if s == 3 and d == j:
                continue
            sign = -1 if d == 0 else 1
            b = fblock(j, sign * s)
            src = foot if (s == 0 and j == 1) else ff.at[b]
            cps.append(send(src, ff.at[b], fr_s.at[d, s, j], fr_r.at[d, s, j], up if d == 0 else down))
        return cps

    def wait_all(cps):
        for cp in cps:
            cp.wait_recv()

    def gather_chips(src, dst, slot):
        cps = []
        for i in range(1, CHIPS):
            cps.append(send(src, dst, chip_s.at[slot, i], chip_r.at[slot, i], peer_chip(i)))
        return cps

    def rows(c, s, lo, hi):
        src = jnp.where(lax.rem(s, 2) == 1, c, CHUNKS)
        dst = jnp.where(lax.rem(s, 2) == 1, CHUNKS, c)
        sub = lax.broadcasted_iota(jnp.int32, (8, CHUNK), 0)
        c0 = y_buf[src, lo] - y_buf[src, lo - 1]
        fd_buf[...] = c0 / flux_den(c0)

        def row(r, carry):
            u = y_buf[src, r]
            cd = y_buf[src, r + 1] - u
            ur = pltpu.roll(u, COLS - 1, 0)
            ur = jnp.concatenate([ur[:-8], jnp.where(sub == 7, 0.0, ur[-8:])], axis=0)
            cr = ur - u
            dd = flux_den(cd)
            dr = flux_den(cr)
            inv = 1.0 / (dd * dr)
            fdn = cd * (dr * inv)
            frt = cr * (dd * inv)
            u0 = u[0:8]
            edge = u0 / flux_den(u0)
            fl = pltpu.roll(frt, 1, 0)
            fl = jnp.concatenate([jnp.where(sub == 0, edge, fl[:8]), fl[8:]], axis=0)
            total = (fdn - fd_buf[...]) + (frt - fl)
            fd_buf[...] = fdn
            new = u + STEP * total
            outside = ((p == 0) & (r < HALO)) | ((p == NPIX - 1) & (r >= HALO + ROWS))
            y_buf[dst, r] = jnp.where(outside, 0.0, new)
            return carry

        lax.fori_loop(lo, hi, row, 0)

    def halves(c):
        def body(r, carry):
            hi, lo = split(y_buf[c, HALO + r])
            ph[c, r] = hi
            plo[c, r] = lo
            return carry

        lax.fori_loop(0, ROWS, body, 0)

    def diffuse(c):
        def substep(s, carry):
            rows(c, s, s, EXT - s)
            return carry

        lax.fori_loop(1, HALO + 1, substep, 0)
        halves(c)

    def diffuse_inner(c):
        def substep(s, carry):
            rows(c, s, HALO + s, HALO + ROWS - s)
            return carry

        lax.fori_loop(1, HALO, substep, 0)

    def diffuse_outer(c):
        def substep(k, carry):
            s = 1 + k // 2
            lo = jnp.where(lax.rem(k, 2) == 0, s, EXT - HALO - s)
            rows(c, s, lo, lo + HALO)
            return carry

        lax.fori_loop(0, 2 * HALO, substep, 0)
        halves(c)

    def flip(c):
        def body(r, carry):
            hi, lo = split(y_buf[c, HALO + r].T)
            pth[r, c * CHUNK : (c + 1) * CHUNK] = hi
            ptl[r, c * CHUNK : (c + 1) * CHUNK] = lo
            return carry

        lax.fori_loop(0, ROWS, body, 0)

    def numerator(c):
        def body(r, acc):
            return acc + dot3(fh8[r], fl8[r], ph[c, r], plo[c, r], 0)

        part = lax.fori_loop(0, ROWS, body, jnp.zeros((RANK, CHUNK), F32), unroll=True)
        np_buf[c] = part.reshape(CHIPS, 2, BLK, CHUNK)

    def rs_core(c):
        return send(np_buf.at[c, :, 1 - core], cr_buf.at[c], core_s.at[c], core_r.at[c], sibling)

    def rs_chips(c, cp):
        cp.wait_recv()
        cr_buf[c] = cr_buf[c] + np_buf[c, :, core]
        cps = []
        for i in range(1, CHIPS):
            cps.append(
                send(
                    cr_buf.at[c, lax.rem(chip + i, CHIPS)], lc_buf.at[c, i],
                    chip_s.at[c, i], chip_r.at[c, i], peer_chip(i),
                )
            )
        return cps

    def ag_chips(c, cps):
        wait_all(cps)
        num = cr_buf[c, chip]
        for i in range(1, CHIPS):
            num = num + lc_buf[c, i]
        new = num * scale_buf[:, c * CHUNK : (c + 1) * CHUNK]
        trace_out[:, c * CHUNK : (c + 1) * CHUNK] = new
        mine = nf.at[chip, core, :, pl.ds(c * CHUNK, CHUNK)]
        mine[...] = new
        return gather_chips(mine, mine, CHUNKS + c)

    def ag_core(c, cps):
        wait_all(cps)
        mine = nf.at[:, core, :, pl.ds(c * CHUNK, CHUNK)]
        return send(mine, mine, core_s.at[CHUNKS + c], core_r.at[CHUNKS + c], sibling)

    def foot_update(c, n, cps):
        wait_all(cps)
        lo, hi = c * CHUNK, (c + n) * CHUNK
        nh, nl = split(nf[:, :, :, lo:hi].reshape(RANK, n * CHUNK))
        first = c == 0

        def put(where, val):
            val = val.reshape(NB, BLK, RANK)
            fn[:, :, where] = val if first else fn[:, :, where] + val

        put(pl.ds(LOCAL, RANK), dot3(nh, nl, nh, nl, 1))

        def body(r, carry):
            put(
                pl.ds(pl.multiple_of(r * COLS, COLS), COLS),
                dot3(nh, nl, pth[r, lo:hi], ptl[r, lo:hi], 0),
            )
            return carry

        lax.fori_loop(0, ROWS, body, 0, unroll=True)

    fx = send(foot, ff.at[t], fx_s.at[0], fx_r.at[0], across)
    own0 = foot_send(0, 1)
    halo_start(0)
    halo_start(1)
    halo_start(2)
    halo_start(3)
    fx.wait_recv()
    oth0 = foot_send(0, 0)
    wait_all(own0)
    own1 = foot_send(1, 1)
    wait_all(oth0)
    oth1 = foot_send(1, 0)
    for cp in loads:
        cp.wait()
    halo_wait(0)
    wait_all(own1)
    own2 = foot_send(2, 1)
    wait_all(oth1)
    oth2 = foot_send(2, 0)
    diffuse(0)
    stores = []

    def store(c):
        cp = pltpu.make_async_copy(
            y_buf.at[c, pl.ds(HALO, ROWS)], den_out.at[:, :, pl.ds(c * CHUNK, CHUNK)], out_sem.at[c]
        )
        cp.start()
        stores.append(cp)

    store(0)
    wait_all(own2)
    own3 = foot_send(3, 1)
    wait_all(oth2)
    oth3 = foot_send(3, 0)
    foot_load.wait()
    trace_load.wait()
    halo_wait(1)
    diffuse(1)
    store(1)
    wait_all(own3)
    wait_all(oth3)

    def split_foot(r, carry):
        hi, lo = split(ff[:, :, pl.ds(pl.multiple_of(r * COLS, COLS), COLS)].reshape(RANK, COLS))
        fh8[r] = hi
        fl8[r] = lo
        return carry

    lax.fori_loop(0, ROWS, split_foot, 0)

    def gram_body(r, acc):
        return acc + dot3(fh8[r], fl8[r], fh8[r], fl8[r], 1)

    gp[...] = lax.fori_loop(0, ROWS, gram_body, jnp.zeros((RANK, RANK), F32), unroll=True).reshape(CHIPS, 2, BLK, RANK)
    gslot = 2 * CHUNKS + 1
    g_core = send(gp.at[:, 1 - core], gcr, core_s.at[gslot], core_r.at[gslot], sibling)
    numerator(0)
    rs0 = rs_core(0)
    numerator(1)
    rs1 = rs_core(1)
    halo_wait(2)
    diffuse(2)
    store(2)
    numerator(2)
    rs2 = rs_core(2)
    diffuse_inner(3)
    flip(0)
    flip(1)
    flip(2)
    halo_wait(3)

    tr = gather_chips(traces, tf.at[chip, core], 2 * CHUNKS)
    g_core.wait_recv()
    gcr[...] = gcr[...] + gp[:, core]
    g_chips = []
    for i in range(1, CHIPS):
        g_chips.append(
            send(gcr.at[lax.rem(chip + i, CHIPS)], gl.at[i], chip_s.at[gslot, i], chip_r.at[gslot, i], peer_chip(i))
        )
    rs0 = rs_chips(0, rs0)
    rs1 = rs_chips(1, rs1)
    rs2 = rs_chips(2, rs2)
    diffuse_outer(3)
    store(3)
    numerator(3)
    rs3 = rs_core(3)
    wait_all(tr)
    tr_core = send(tf.at[:, core], tf.at[:, core], core_s.at[2 * CHUNKS], core_r.at[2 * CHUNKS], sibling)
    wait_all(g_chips)
    gram = gcr[chip]
    for i in range(1, CHIPS):
        gram = gram + gl[i]
    rs3 = rs_chips(3, rs3)
    flip(3)
    tr_core.wait_recv()
    gh, gl_ = split(gram)
    th, tl = split(tf[...].reshape(RANK, FRAMES))
    scale_buf[...] = tf[chip, core] / dot3(gh, gl_, th, tl, 0)
    ag0 = ag_chips(0, rs0)
    ag1 = ag_chips(1, rs1)
    ag2 = ag_chips(2, rs2)
    ag3 = ag_chips(3, rs3)
    ag0 = ag_core(0, ag0)
    ag1 = ag_core(1, ag1)
    ag2 = ag_core(2, ag2)
    foot_update(0, 2, (ag0, ag1))
    foot_update(2, 1, (ag2,))
    ag3 = ag_core(3, ag3)
    foot_update(3, 1, (ag3,))

    def low(ref, b):
        return ref.at[b, :, pl.ds(0, PART)]

    def ring_send(s, j, got):
        cps = []
        for d in range(2):
            if s == 0 and d == j:
                continue
            land = lu if d == 0 else ld
            b = fblock(j, (NZ // 2 - s) * (1 if d == 0 else -1))
            if d in got:
                land[s - 1, j] = land[s - 1, j] + fn[b, :, :PART]
                src = land.at[s - 1, j]
            else:
                src = low(fn, b)
            cps.append(send(src, land.at[s, j], ring_s.at[d, s, j], ring_r.at[d, s, j], up if d == 0 else down))
        return cps

    sent = list(pending)
    pending.clear()
    cross = {}
    for dz in (4, 3, -3, 2, -2, 1, -1, 0):
        k = dz % NZ
        cross[dz] = send(
            fn.at[fblock(0, dz), :, pl.ds(PART, REST)], xb.at[k], rx_s.at[k], rx_r.at[k], across
        )

    def take(dz):
        cross[dz].wait_recv()
        k = dz % NZ
        xb[k] = xb[k] + fn[fblock(1, dz), :, PART:]

    def rest_send(s, cps):
        if s == 0:
            take(4)
        else:
            take(4 - s)
            take(s - 4)
            wait_all(cps)
        out = []
        for d in range(2):
            land = lub if d == 0 else ldb
            k = ((4 - s) * (1 if d == 0 else -1)) % NZ
            w = pl.ds(d * (REST // 2), REST // 2) if s <= 1 else pl.ds(0, REST)
            if s > 0:
                xb[k, :, w] = xb[k, :, w] + land[s - 1, :, w]
            w = w if s == 0 else pl.ds(0, REST)
            out.append(
                send(xb.at[k, :, w], land.at[s, :, w], rest_s.at[d, s], rest_r.at[d, s], up if d == 0 else down)
            )
        return out

    r0 = ring_send(0, 0, ())
    r1 = ring_send(0, 1, ())
    for cp in sent:
        cp.wait_send()
    for c in range(CHUNKS):
        halo_wait_send(c)
    for cp in stores:
        cp.wait()
    rb = rest_send(0, ())
    for s in range(1, 4):
        wait_all(r0)
        r0 = ring_send(s, 0, (1,) if s == 1 else (0, 1))
        wait_all(r1)
        r1 = ring_send(s, 1, (0,) if s == 1 else (0, 1))
        rb = rest_send(s, rb)
    wait_all(r0)
    lu[3, 0] = (lu[3, 0] + ld[3, 0]) + fn[fblock(0, 0), :, :PART]
    rx = send(lu.at[3, 0], lx, rx_s.at[NZ], rx_r.at[NZ], across)
    wait_all(r1)
    lu[3, 1] = (lu[3, 1] + ld[3, 1]) + fn[fblock(1, 0), :, :PART]
    take(0)
    wait_all(rb)
    xb[0] = xb[0] + (lub[3] + ldb[3])
    kh, kl = split(xb[0, :, LOCAL - PART :])

    def final(r):
        w = slice(r * COLS, (r + 1) * COLS)
        den = dot3(kh, kl, fh8[r], fl8[r], 0)
        if w.start >= PART:
            num = xb[0, :, w.start - PART : w.stop - PART]
        else:
            num = lu[3, 1, :, w] + lx[:, w]
        foot_out[:, w] = ff[t, :, w] * num / den

    for r in range(PART // COLS, ROWS):
        final(r)
    rx.wait_recv()
    for r in range(PART // COLS):
        final(r)

    for cp in pending:
        cp.wait_send()


def move_out(den, foot, trace, den_hbm, foot_hbm, trace_hbm, sems):
    cps = [pltpu.make_async_copy(den.at[r], den_hbm.at[r], sems.at[r]) for r in range(ROWS)]
    cps.append(pltpu.make_async_copy(foot, foot_hbm, sems.at[ROWS]))
    cps.append(pltpu.make_async_copy(trace, trace_hbm, sems.at[ROWS + 1]))
    for cp in cps:
        cp.start()
    for cp in cps:
        cp.wait()


def stay(x):
    return pltpu.with_memory_space_constraint(x, pltpu.MemorySpace.HBM)


def body(raw_movie, footprints, traces):
    dma = pltpu.SemaphoreType.DMA
    vm = pltpu.VMEM
    hbm = pl.BlockSpec(memory_space=pltpu.MemorySpace.HBM)
    inv = pl.BlockSpec(memory_space=pltpu.MemorySpace.VMEM)
    outs = pl.pallas_call(
        kernel,
        out_shape=(
            jax.ShapeDtypeStruct(raw_movie.shape, F32),
            jax.ShapeDtypeStruct(footprints.shape, F32),
            jax.ShapeDtypeStruct(traces.shape, F32),
        ),
        in_specs=[hbm, hbm, hbm],
        out_specs=(inv, inv, inv),
        scratch_shapes=[
            vm((CHUNKS + 1, EXT, COLS, CHUNK), F32),
            vm((COLS, CHUNK), F32),
            vm((CHUNKS, ROWS, COLS, CHUNK), BF16),
            vm((CHUNKS, ROWS, COLS, CHUNK), BF16),
            vm((NB, BLK, LOCAL), F32),
            vm((ROWS, RANK, COLS), BF16),
            vm((ROWS, RANK, COLS), BF16),
            vm((NB, BLK, WIDE), F32),
            vm((4, 2, BLK, PART), F32),
            vm((4, 2, BLK, PART), F32),
            vm((BLK, PART), F32),
            vm((CHIPS, 2, BLK, RANK), F32),
            vm((CHIPS, BLK, RANK), F32),
            vm((CHIPS, BLK, RANK), F32),
            vm((CHIPS, 2, BLK, FRAMES), F32),
            vm((BLK, FRAMES), F32),
            vm((CHUNKS, CHIPS, 2, BLK, CHUNK), F32),
            vm((CHUNKS, CHIPS, BLK, CHUNK), F32),
            vm((CHUNKS, CHIPS, BLK, CHUNK), F32),
            vm((CHIPS, 2, BLK, FRAMES), F32),
            vm((ROWS, FRAMES, COLS), BF16),
            vm((ROWS, FRAMES, COLS), BF16),
            vm((NZ, BLK, REST), F32),
            vm((4, BLK, REST), F32),
            vm((4, BLK, REST), F32),
            dma((CHUNKS + 2,)),
            dma((CHUNKS,)),
            dma((2, CHUNKS)),
            dma((2, CHUNKS)),
            dma((1,)),
            dma((1,)),
            dma((2, 4, 2)),
            dma((2, 4, 2)),
            dma((2, 4, 2)),
            dma((2, 4, 2)),
            dma((NZ + 1,)),
            dma((NZ + 1,)),
            dma((2 * CHUNKS + 2,)),
            dma((2 * CHUNKS + 2,)),
            dma((2 * CHUNKS + 2, CHIPS)),
            dma((2 * CHUNKS + 2, CHIPS)),
            dma((2, 4)),
            dma((2, 4)),
        ],
        compiler_params=pltpu.CompilerParams(
            collective_id=0, has_side_effects=True, vmem_limit_bytes=48 * 1024 * 1024
        ),
        cost_estimate=pl.CostEstimate(flops=4 * 10**9, bytes_accessed=16 * 2**20, transcendentals=0),
    )(raw_movie, stay(footprints), stay(traces))
    return pl.pallas_call(
        move_out,
        out_shape=tuple(jax.ShapeDtypeStruct(o.shape, F32) for o in outs),
        in_specs=[inv, inv, inv],
        out_specs=(hbm, hbm, hbm),
        scratch_shapes=[dma((ROWS + 2,))],
        compiler_params=pltpu.CompilerParams(vmem_limit_bytes=8 * 1024 * 1024),
    )(*outs)


def solution(mesh):
    placed = (P("pix", None, "tm"), P("tm", "pix"), P("pix", "tm"))
    return jax.shard_map(body, mesh=mesh, in_specs=placed, out_specs=placed, check_vma=False)
```
